32 devices in a mesh: grp: 2 (over y), ep: 4 (over z), tp: 4 (over x, core).
Axes of the slice: x: 2, y: 2, z: 4, core: 2. Of those that a mesh axis runs over, the one named last changes fastest.
Arguments:
- question_q: bfloat16 [1024, 32, 128], P(('grp', 'ep'), 'tp'), parts along dimension 0, may hold values from -125 to 125
- question_kv: bfloat16 [1024, 4, 2, 128], P(('grp', 'ep')), parts along dimension 0, may hold values from -6 to 6
- doc_kv: bfloat16 [16, 128, 4, 2, 128], P(('grp', 'ep')), parts along dimension 0, may hold values from -6 to 6
- doc_lens: int32 [16], P('grp'), parts along dimension 0, may hold values from 1 to 128, as said below
- query_docs: int32 [8, 4], P('grp'), parts along dimension 0, may hold values from 0 to 7, as said below
- ctx_pos: int32 [8, 5], P('grp'), parts along dimension 0, may hold values from 0 to 827, as said below
- hidden: bfloat16 [1024, 4096], P(('grp', 'ep'), 'tp'), parts along dimension 0, may hold values from -1.5 to 1.5
- out_proj: bfloat16 [4096, 4096], P('ep', 'tp'), may hold values from -0.0234375 to 0.0234375
- norm_gain: bfloat16 [4096], P('tp'), may hold values from 0.5 to 1.5
- router_weight: bfloat16 [4096, 16], P('tp'), may hold values from -0.046875 to 0.046875
- w_gate_up: bfloat16 [16, 4096, 2, 1024], P('ep', 'tp'), may hold values from -0.09375 to 0.09375
- w_down: bfloat16 [16, 1024, 4096], P('ep', None, 'tp'), may hold values from -0.1875 to 0.1875
- expert_ids: int32 [1024, 8], P(('grp', 'ep')), parts along dimension 0, may hold values from 0 to 15, all different within a row; in each aligned block of 128 rows (0 to 127, 128 to 255, ...) at most 64 rows name the same one
Outputs:
- layer_out: bfloat16 [1024, 4096], P(('grp', 'ep'), 'tp'), parts along dimension 0
The draws below stay inside these ranges and needn't reach their ends.
There are 2 independent parts, one for each index of `grp`. The reference program is written for one: setup_inputs(seed, part) draws one part's arguments, and reference() takes and returns one part's arrays. A program takes and returns all parts, laid end to end along the dimension named above; an argument that names none is the same for every part. Nothing has to cross between parts.
Inputs may be any that keep to these rules, and one draw needn't show every extreme that they name: `doc_lens`: document d is held at row d of doc_kv; some document of some query's list has exactly 128 tokens. `query_docs`: the 4 documents of a query lie in 4 different blocks of 2 consecutive documents. `ctx_pos`: in each row, every entry is at least the one before it plus the length of the document before it. `expert_ids`: each query's 128 tokens name every expert exactly 64 times.
All inputs are finite; a program needn't handle non-finite values.
Results may differ from the reference program's by a relative error of at most 0.017.
Values may be sent and summed in bfloat16 or wider, within the bound.
A program may use at most 128 MiB of HBM per device.

```python
import math
import jax
import jax.numpy as jnp
import numpy as np
from jax import lax

D = 4096
QH = 32
KVH = 4
HD = 128
HID = 1024
TOP = 8
QLEN = 128
DOC_MAX = 128
POOL_DEV = 2
EXPERTS = 16
CAP = 64
DPQ = 4
QUERIES = 4
TOKENS = 512
POOL_DOCS = 8
N_TP = 4


def pool_plan(key):
    base = jax.random.fold_in(key, 11)
    owner_key, local_key, length_key, gap_key = jax.random.split(base, 4)
    owners_all = POOL_DOCS // POOL_DEV
    scores = jax.random.randint(owner_key, (QUERIES, owners_all), 0, 1 << 20) * owners_all + jnp.arange(owners_all, dtype=jnp.int32)[None, :]
    owners = jnp.argsort(scores, axis=1)[:, :DPQ].astype(jnp.int32)
    local = jax.random.randint(local_key, (QUERIES, DPQ), 0, POOL_DEV)
    docs = owners * POOL_DEV + local
    lengths = jax.random.randint(length_key, (POOL_DOCS,), 1, DOC_MAX + 1)
    lengths = lengths.at[docs[0]].set(DOC_MAX)
    gaps = jax.random.randint(gap_key, (QUERIES, DPQ + 1), 0, 64)
    gaps = gaps.at[0].set(63)
    spans = jnp.concatenate([jnp.zeros((QUERIES, 1), jnp.int32), lengths[docs]], axis=1)
    positions = jnp.cumsum(gaps + spans, axis=1).astype(jnp.int32)
    return (docs.astype(jnp.int32), lengths.astype(jnp.int32), positions)


def draw_doc_lens(key, part):
    return pool_plan(key)[1]


def draw_query_docs(key, part):
    return pool_plan(key)[0]


def draw_ctx_pos(key, part):
    return pool_plan(key)[2]


def draw_question_q(key, part):
    shape = (TOKENS, QH, HD)
    base_key = jax.random.fold_in(jax.random.fold_in(key, 3), 0)
    values = jnp.clip(3.0 * jax.random.normal(base_key, shape, jnp.float32), -12.0, 12.0)
    return values.astype(jnp.bfloat16)


def level_of(stream_key, dims, pieces, least, largest):
    loudness = 1.0
    for dim, shards_of in pieces:
        heights = jax.random.uniform(jax.random.fold_in(jax.random.fold_in(stream_key, 6), dim), (shards_of,), jnp.float32, least / len(pieces), largest / len(pieces))
        loudness = loudness * jnp.repeat(jnp.exp(heights), dims[dim] // shards_of).reshape((-1,) + (1,) * (len(dims) - 1 - dim))
    return loudness


def shared_out(rng, own, number, rows, count, top, reach, lean):
    ranking = jax.random.permutation(rng, count)
    heavy_load, common = portions_of(count, rows * top, reach, lean, True), portions_of(count, rows * top, reach, lean, False)
    places = jnp.arange(count)

    def named(sizes, offset_by):
        used = int((sizes > 0).sum())
        fixed = max(1, used // 4)
        passed = fixed + (places - fixed + offset_by * (used - fixed)) % max(1, count - fixed)
        return jnp.zeros((count,), jnp.int32).at[ranking[jnp.where(places < fixed, places, passed)]].set(jnp.asarray(sizes, jnp.int32))

    sizes = jnp.where(number % 4 == 0, named(heavy_load, number // 4), named(common, number - number // 4 - 1))
    mixed = jax.random.permutation(jax.random.fold_in(own, 3), count)
    donor, receiver = mixed[0:count // 2 * 2:2], mixed[1:count // 2 * 2:2]
    slack = jnp.minimum(sizes[donor] - 1, reach - sizes[receiver]) // 2
    slack = jnp.where((donor == ranking[0]) | (receiver == ranking[0]) | (sizes[receiver] == 0), 0, jnp.maximum(slack, 0))
    passed = jax.random.randint(jax.random.fold_in(own, 4), (count // 2,), 0, 1 << 20) % (slack + 1)
    sizes = sizes.at[donor].add(-passed).at[receiver].add(passed)
    members = jnp.searchsorted(jnp.cumsum(sizes), jnp.arange(rows * top), side="right").astype(jnp.int32)
    grid = members.reshape(top, rows).T
    grid = grid[jax.random.permutation(jax.random.fold_in(own, 1), rows)]
    offset_by = jax.random.randint(jax.random.fold_in(own, 2), (rows, 1), 0, top)
    return jnp.take_along_axis(grid, (jnp.arange(top)[None, :] + offset_by) % top, axis=1)


def portions_of(number_of, total, limit, lean, full):
    weights = [(1 << 20) // math.isqrt(grade ** lean) + 1 for grade in range(1, number_of + 1)]
    largest = limit if full else min(limit, max(-(-total // number_of), total * weights[0] // sum(weights)))
    least = 1 if total - largest >= number_of - 1 else 0
    given, surplus = [largest] + [least] * (number_of - 1), total - largest - least * (number_of - 1)
    while surplus > 0:
        candidates = [i for i in range(1, number_of) if given[i] < largest] or [i for i in range(1, number_of) if given[i] < limit]
        pool, budget = sum([weights[i] for i in candidates]), surplus
        for i in candidates:
            extra = min(limit - given[i], max(1, budget * weights[i] // pool), surplus)
            given[i] = given[i] + extra
            surplus = surplus - extra
    return np.array(given)


def bell_draw(rng, shape, scale, limit, shards=(), kind=jnp.bfloat16):
    level = level_of(rng, shape, shards, -0.22, 0.18) if shards else 1.0
    values = jax.random.normal(rng, shape, jnp.float32) * scale * level
    return jnp.minimum(jnp.maximum(values, -limit), limit).astype(kind)


def setup_inputs(seed: int = 0, part: int = 0) -> dict:
    splits = jax.random.split(jax.random.key(seed), 14)
    part_keys = jax.random.split(jax.random.fold_in(splits[13], part), 14)
    question_q = draw_question_q(jax.random.fold_in(jax.random.fold_in(splits[13], part), 71), part)
    question_kv = bell_draw(part_keys[1], (TOKENS, KVH, 2, HD), 1.0, 6.0, ((0, 4),))
    doc_kv = bell_draw(part_keys[2], (POOL_DOCS, DOC_MAX, KVH, 2, HD), 1.0, 6.0, ((0, 4),))
    doc_lens = draw_doc_lens(jax.random.fold_in(jax.random.fold_in(splits[13], part), 71), part)
    query_docs = draw_query_docs(jax.random.fold_in(jax.random.fold_in(splits[13], part), 71), part)
    ctx_pos = draw_ctx_pos(jax.random.fold_in(jax.random.fold_in(splits[13], part), 71), part)
    hidden = bell_draw(part_keys[6], (TOKENS, D), 0.25, 1.5, ((0, 4), (1, 4)))
    out_proj = bell_draw(splits[7], (QH * HD, D), (16 * QH * HD) ** -0.5, 0.0234375, ((0, 4), (1, 4)))
    norm_gain = jnp.clip(1.0 + 0.1 * jax.random.normal(splits[8], (D,), jnp.float32), 0.5, 1.5).astype(jnp.bfloat16)
    router_weight = bell_draw(splits[9], (D, EXPERTS), (4 * D) ** -0.5, 0.046875, ((0, 4),))
    w_gate_up = bell_draw(splits[10], (EXPERTS, D, 2, HID), D ** -0.5, 0.09375, ((0, 4), (1, 4)))
    w_down = bell_draw(splits[11], (EXPERTS, HID, D), HID ** -0.5, 0.1875, ((0, 4), (2, 4)))
    expert_ids_keys = jax.random.split(jax.random.fold_in(part_keys[12], 1), TOKENS // QLEN)
    expert_ids_turns = jax.random.permutation(jax.random.fold_in(part_keys[12], 3), TOKENS // QLEN)
    expert_ids = jax.vmap(lambda own, number: shared_out(jax.random.fold_in(part_keys[12], 2), own, number, QLEN, EXPERTS, TOP, CAP, 0))(expert_ids_keys, expert_ids_turns).reshape((TOKENS, TOP))
    return {"question_q": question_q, "question_kv": question_kv, "doc_kv": doc_kv, "doc_lens": doc_lens, "query_docs": query_docs, "ctx_pos": ctx_pos, "hidden": hidden, "out_proj": out_proj, "norm_gain": norm_gain, "router_weight": router_weight, "w_gate_up": w_gate_up, "w_down": w_down, "expert_ids": expert_ids}


rope_theta = 1000000.0
norm_eps = 1e-06

def narrow(values):
    return lax.optimization_barrier(values.astype(jnp.bfloat16))

def rotate(values, positions):
    half = values.shape[-1] // 2
    freq = jnp.exp(jnp.arange(half, dtype=jnp.float32) * (-2.0 * math.log(rope_theta) / values.shape[-1]))
    angle = positions.astype(jnp.float32)[:, None] * freq[None, :]
    shape = (values.shape[0],) + (1,) * (values.ndim - 2) + (half,)
    cosine = jnp.cos(angle).reshape(shape)
    sine = jnp.sin(angle).reshape(shape)
    floats = values.astype(jnp.float32)
    first = floats[..., :half]
    second = floats[..., half:]
    return jnp.concatenate([first * cosine - second * sine, second * cosine + first * sine], axis=-1)

def attend(q_rows, kv_rows, context, lengths, starts):
    doc_pos = jnp.repeat(starts[:DPQ], DOC_MAX, total_repeat_length=DPQ * DOC_MAX)
    doc_keys = rotate(context[:, :, :, 0].reshape(DPQ * DOC_MAX, KVH, HD), doc_pos).astype(jnp.bfloat16)
    doc_values = context[:, :, :, 1].reshape(DPQ * DOC_MAX, KVH, HD)
    question_pos = starts[DPQ] + jnp.arange(QLEN, dtype=jnp.int32)
    queries = rotate(q_rows, question_pos).astype(jnp.bfloat16)
    own_keys = rotate(kv_rows[:, :, 0], question_pos).astype(jnp.bfloat16)
    keys = jnp.concatenate([doc_keys, own_keys], axis=0)
    values = jnp.concatenate([doc_values, kv_rows[:, :, 1]], axis=0)
    valid = (jnp.arange(DOC_MAX, dtype=jnp.int32)[None, :] < lengths[:, None]).reshape(DPQ * DOC_MAX)
    causal = jnp.arange(QLEN)[:, None] >= jnp.arange(QLEN)[None, :]
    allowed = jnp.concatenate([jnp.broadcast_to(valid[None, :], (QLEN, DPQ * DOC_MAX)), causal], axis=1)
    grouped = queries.reshape(QLEN, KVH, QH // KVH, HD)
    scores = jnp.einsum('ighd,jgd->ghij', grouped.astype(jnp.float32), keys.astype(jnp.float32)) * HD ** (-0.5)
    scores = jnp.where(allowed[None, None], scores, -jnp.inf)
    ceiling = lax.optimization_barrier(jnp.max(scores, axis=-1, keepdims=True))
    probs = jnp.exp(scores - ceiling)
    denominator = lax.optimization_barrier(jnp.sum(probs, axis=-1, keepdims=True))
    mixed = jnp.einsum('ghij,jgd->ghid', narrow(probs).astype(jnp.float32), values.astype(jnp.float32)) / denominator
    return jnp.transpose(mixed, (2, 0, 1, 3)).reshape(QLEN, QH * HD).astype(jnp.bfloat16)

def reference(question_q, question_kv, doc_kv, doc_lens, query_docs, ctx_pos, hidden, out_proj, norm_gain, router_weight, w_gate_up, w_down, expert_ids):

    def one_query(index):
        q_rows = lax.dynamic_slice_in_dim(question_q, index * QLEN, QLEN, 0)
        kv_rows = lax.dynamic_slice_in_dim(question_kv, index * QLEN, QLEN, 0)
        docs = query_docs[index]
        return attend(q_rows, kv_rows, doc_kv[docs], doc_lens[docs], ctx_pos[index])
    attended = lax.map(one_query, jnp.arange(QUERIES, dtype=jnp.int32)).reshape(TOKENS, QH * HD)
    projected = jnp.dot(attended, out_proj, preferred_element_type=jnp.float32)
    residual = narrow(hidden.astype(jnp.float32) + projected).astype(jnp.float32)
    gain = norm_gain.astype(jnp.float32)
    inv_rms = lax.rsqrt(lax.optimization_barrier(jnp.mean(residual * residual, axis=1)) + norm_eps)
    normed = narrow(residual * inv_rms[:, None] * gain[None, :])
    logits = jnp.dot(residual * gain[None, :], router_weight.astype(jnp.float32), precision=lax.Precision.HIGHEST) * inv_rms[:, None]
    mix = jax.nn.softmax(jnp.take_along_axis(logits, expert_ids, axis=1), axis=1)
    flat = expert_ids.reshape(TOKENS * TOP)
    per_expert = QUERIES * CAP

    def one_expert(expert):
        rows = jnp.nonzero(flat == expert, size=per_expert)[0].astype(jnp.int32)
        inputs = jnp.take(normed, rows // TOP, axis=0).astype(jnp.float32).reshape(per_expert, N_TP, D // N_TP)
        weights = w_gate_up[expert].astype(jnp.float32).reshape(N_TP, D // N_TP, 2 * HID)
        parts = narrow(jnp.einsum('rbd,bdh->brh', inputs, weights)).astype(jnp.float32)
        summed = lax.optimization_barrier(jnp.sum(parts, axis=0))
        activated = (jax.nn.silu(summed[:, :HID]) * summed[:, HID:]).astype(jnp.bfloat16)
        output = jnp.dot(activated, w_down[expert], preferred_element_type=jnp.float32).astype(jnp.bfloat16)
        return (rows, output)
    rows, outputs = lax.map(one_expert, jnp.arange(EXPERTS, dtype=jnp.int32))
    gathered = jnp.zeros((TOKENS * TOP, D), jnp.bfloat16).at[rows.reshape(-1)].set(outputs.reshape(-1, D))
    combined = jnp.einsum('tk,tkd->td', mix, gathered.reshape(TOKENS, TOP, D).astype(jnp.float32))
    return (residual + combined).astype(jnp.bfloat16)
```

```python
import math

import jax
import jax.numpy as jnp
from jax import lax
from jax.sharding import PartitionSpec as P

D = 4096
HID = 1024


rope_theta = 1000000.0
norm_eps = 1e-06


def narrow(values):
    return lax.optimization_barrier(values.astype(jnp.bfloat16))


def rotate(values, positions):
    half = values.shape[-1] // 2
    freq = jnp.exp(
        jnp.arange(half, dtype=jnp.float32) * (-2.0 * math.log(rope_theta) / values.shape[-1])
    )
    angle = positions.astype(jnp.float32)[:, None] * freq[None, :]
    shape = (values.shape[0],) + (1,) * (values.ndim - 2) + (half,)
    cosine = jnp.cos(angle).reshape(shape)
    sine = jnp.sin(angle).reshape(shape)
    floats = values.astype(jnp.float32)
    first = floats[..., :half]
    second = floats[..., half:]
    return jnp.concatenate(
        [first * cosine - second * sine, second * cosine + first * sine], axis=-1
    )


def fetch_context(doc_kv, doc_lens, query_docs, row_pos, device, kv_pick):
    pool_dev, doc_max, kv_heads, pair, head_dim = doc_kv.shape
    docs_per = query_docs.shape[1]
    pool_head = lax.dynamic_index_in_dim(doc_kv, kv_pick, 2, keepdims=False).reshape(
        pool_dev, doc_max, pair * head_dim
    )
    held = device * pool_dev + jnp.arange(pool_dev, dtype=jnp.int32)
    wanted = jnp.sum((query_docs[:, :, None] == held[None, None, :]).astype(jnp.float32), axis=1)
    sending = jnp.einsum(
        "rl,lkc->rkc", wanted.astype(jnp.bfloat16), pool_head, preferred_element_type=jnp.float32
    ).astype(jnp.bfloat16)
    received = lax.all_to_all(sending, "ep", split_axis=0, concat_axis=0, tiled=True)
    my_docs = lax.dynamic_index_in_dim(query_docs, device, 0, keepdims=False)
    context = jnp.take(received, my_docs // pool_dev, axis=0)
    lengths = jnp.take(doc_lens, my_docs)
    positions = jnp.repeat(row_pos[:docs_per], doc_max, total_repeat_length=docs_per * doc_max)
    keys = rotate(context[:, :, :head_dim].reshape(docs_per * doc_max, head_dim), positions).astype(
        jnp.bfloat16
    )
    values = context[:, :, head_dim:].reshape(docs_per * doc_max, head_dim)
    valid = (jnp.arange(doc_max, dtype=jnp.int32)[None, :] < lengths[:, None]).reshape(
        docs_per * doc_max
    )
    return (keys, values, valid)


def project(attended, out_proj):
    lanes = lax.axis_size("tp")
    groups = lax.axis_size("ep")
    length = attended.shape[0]
    if lanes == groups:
        swap = [(e * lanes + t, t * lanes + e) for e in range(groups) for t in range(lanes)]
        block = lax.ppermute(attended, ("ep", "tp"), swap)
        tokens = lax.all_gather(block, "tp", axis=0, tiled=True)
    else:
        all_heads = lax.all_gather(attended, "tp", axis=1, tiled=True)
        split = jnp.swapaxes(all_heads.reshape(length, groups, -1), 0, 1)
        tokens = lax.all_to_all(split, "ep", split_axis=0, concat_axis=0, tiled=True)
        tokens = tokens.reshape(groups * length, -1)
    part = jnp.dot(tokens, out_proj, preferred_element_type=jnp.float32)
    return lax.psum_scatter(
        part.astype(jnp.bfloat16), "ep", scatter_dimension=0, tiled=True
    ).astype(jnp.float32)


def per_device(
    question_q,
    question_kv,
    doc_kv,
    doc_lens,
    query_docs,
    ctx_pos,
    hidden,
    out_proj,
    norm_gain,
    router_weight,
    w_gate_up,
    w_down,
    expert_ids,
):
    lanes = lax.axis_size("tp")
    groups = lax.axis_size("ep")
    lane = lax.axis_index("tp")
    device = lax.axis_index("ep")
    length, heads_here, head_dim = question_q.shape
    kv_heads = question_kv.shape[1]
    kv_pick = lane * kv_heads // lanes
    scale = head_dim ** (-0.5)
    docs_per = query_docs.shape[1]
    row_pos = lax.dynamic_index_in_dim(ctx_pos, device, 0, keepdims=False)
    question_pos = row_pos[docs_per] + jnp.arange(length, dtype=jnp.int32)
    queries = rotate(question_q, question_pos).astype(jnp.bfloat16)
    own_kv = lax.dynamic_index_in_dim(question_kv, kv_pick, 1, keepdims=False)
    own_keys = rotate(own_kv[:, 0], question_pos).astype(jnp.bfloat16)
    own_values = own_kv[:, 1]
    causal = jnp.arange(length)[:, None] >= jnp.arange(length)[None, :]
    doc_keys, doc_values, valid = fetch_context(
        doc_kv, doc_lens, query_docs, row_pos, device, kv_pick
    )
    keys = jnp.concatenate([doc_keys, own_keys], axis=0)
    values = jnp.concatenate([doc_values, own_values], axis=0)
    allowed = jnp.concatenate(
        [jnp.broadcast_to(valid[None, :], (length, valid.shape[0])), causal], axis=1
    )
    scores = jnp.einsum("ihd,jd->hij", queries, keys, preferred_element_type=jnp.float32) * scale
    scores = jnp.where(allowed[None], scores, -jnp.inf)
    ceiling = jnp.max(scores, axis=-1, keepdims=True)
    probs = jnp.exp(scores - ceiling)
    denominator = jnp.sum(probs, axis=-1, keepdims=True)
    mixed = jnp.einsum(
        "hij,jd->hid", probs.astype(jnp.bfloat16), values, preferred_element_type=jnp.float32
    )
    attended = (
        jnp.transpose(mixed / denominator, (1, 0, 2))
        .reshape(length, heads_here * head_dim)
        .astype(jnp.bfloat16)
    )
    width_here = hidden.shape[1]
    projected = project(attended, out_proj)
    residual_wide = narrow(hidden.astype(jnp.float32) + projected).astype(jnp.float32)
    gain = norm_gain.astype(jnp.float32)
    squares, logit_part = lax.psum(
        (
            jnp.sum(residual_wide * residual_wide, axis=1),
            jnp.dot(
                residual_wide * gain[None, :],
                router_weight.astype(jnp.float32),
                precision=lax.Precision.HIGHEST,
            ),
        ),
        "tp",
    )
    inv_rms = lax.rsqrt(squares / D + norm_eps)
    normed = (residual_wide * inv_rms[:, None] * gain[None, :]).astype(jnp.bfloat16)
    logits = logit_part * inv_rms[:, None]
    mix = jax.nn.softmax(jnp.take_along_axis(logits, expert_ids, axis=1), axis=1)
    local_experts = w_gate_up.shape[0]
    capacity = length * expert_ids.shape[1] // (local_experts * groups)
    ids_all = lax.all_gather(expert_ids, "ep", axis=0)
    local = device * local_experts + jnp.arange(local_experts, dtype=jnp.int32)
    names = ids_all[:, :, :, None] == local
    member = jnp.any(names, axis=2)
    earlier = jnp.arange(length)[:, None] > jnp.arange(length)[None, :]
    rank = jnp.einsum(
        "nm,sme->sen",
        earlier.astype(jnp.bfloat16),
        member.astype(jnp.bfloat16),
        preferred_element_type=jnp.float32,
    )
    seat = jnp.where(jnp.swapaxes(member, 1, 2), rank.astype(jnp.int32), -1)
    picks = (seat[:, :, None, :] == jnp.arange(capacity, dtype=jnp.int32)[:, None]).astype(
        jnp.bfloat16
    )
    normed_all = lax.all_gather(normed, "ep", axis=0)
    mix_all = lax.all_gather(mix, "ep", axis=0)
    share = jnp.sum(jnp.where(names, mix_all[:, :, :, None], 0.0), axis=2)
    share = jnp.swapaxes(share, 1, 2)
    arrived = jnp.einsum(
        "secn,snd->escd", picks, normed_all, preferred_element_type=jnp.float32
    ).astype(jnp.bfloat16)
    rows = groups * capacity
    arrived = arrived.reshape(local_experts, rows, width_here)
    hidden_here = HID // lanes
    term = jnp.einsum("erd,edgh->hegr", arrived, w_gate_up, preferred_element_type=jnp.float32)
    summed = lax.psum_scatter(
        term.astype(jnp.bfloat16), "tp", scatter_dimension=0, tiled=True
    ).astype(jnp.float32)
    activated = (jax.nn.silu(summed[:, :, 0]) * summed[:, :, 1]).astype(jnp.bfloat16)
    piece = lax.all_gather(activated, "tp", axis=0, tiled=True)
    expert_out = jnp.einsum(
        "her,ehd->erd", piece, w_down, preferred_element_type=jnp.float32
    ).astype(jnp.bfloat16)
    share_high = share.astype(jnp.bfloat16)
    share_low = (share - share_high.astype(jnp.float32)).astype(jnp.bfloat16)
    weights = jnp.stack([picks * share_high[:, :, None, :], picks * share_low[:, :, None, :]])
    partial = jnp.einsum(
        "psecn,escd->snd",
        weights,
        expert_out.reshape(local_experts, groups, capacity, width_here),
        preferred_element_type=jnp.float32,
    )
    combined = lax.psum_scatter(
        partial.astype(jnp.bfloat16).reshape(groups * length, width_here),
        "ep",
        scatter_dimension=0,
        tiled=True,
    )
    return (residual_wide + combined.astype(jnp.float32)).astype(jnp.bfloat16)


def solution(mesh):
    placed = (
        P(("grp", "ep"), "tp", None),
        P(("grp", "ep"), None, None, None),
        P(("grp", "ep"), None, None, None, None),
        P("grp"),
        P("grp", None),
        P("grp", None),
        P(("grp", "ep"), "tp"),
        P("ep", "tp"),
        P("tp"),
        P("tp", None),
        P("ep", "tp", None, None),
        P("ep", None, "tp"),
        P(("grp", "ep"), None),
    )
    return jax.shard_map(
        per_device, mesh=mesh, in_specs=placed, out_specs=P(("grp", "ep"), "tp"), check_vma=False
    )
```

```python
import math

import jax
import jax.numpy as jnp
from jax import lax
from jax.experimental import pallas as pl
from jax.experimental.pallas import tpu as pltpu
from jax.sharding import PartitionSpec as P

D = 4096
HID = 1024


rope_theta = 1000000.0
norm_eps = 1e-06


def narrow(values):
    return lax.optimization_barrier(values.astype(jnp.bfloat16))


def rotate(values, positions):
    half = values.shape[-1] // 2
    freq = jnp.exp(
        jnp.arange(half, dtype=jnp.float32) * (-2.0 * math.log(rope_theta) / values.shape[-1])
    )
    angle = positions.astype(jnp.float32)[:, None] * freq[None, :]
    shape = (values.shape[0],) + (1,) * (values.ndim - 2) + (half,)
    cosine = jnp.cos(angle).reshape(shape)
    sine = jnp.sin(angle).reshape(shape)
    floats = values.astype(jnp.float32)
    first = floats[..., :half]
    second = floats[..., half:]
    return jnp.concatenate(
        [first * cosine - second * sine, second * cosine + first * sine], axis=-1
    )


def fetch_context(doc_kv, doc_lens, query_docs, row_pos, device, kv_pick):
    pool_dev, doc_max, kv_heads, pair, head_dim = doc_kv.shape
    docs_per = query_docs.shape[1]
    pool_head = lax.dynamic_index_in_dim(doc_kv, kv_pick, 2, keepdims=False).reshape(
        pool_dev, doc_max, pair * head_dim
    )
    held = device * pool_dev + jnp.arange(pool_dev, dtype=jnp.int32)
    wanted = jnp.sum((query_docs[:, :, None] == held[None, None, :]).astype(jnp.float32), axis=1)
    sending = jnp.einsum(
        "rl,lkc->rkc", wanted.astype(jnp.bfloat16), pool_head, preferred_element_type=jnp.float32
    ).astype(jnp.bfloat16)
    received = lax.all_to_all(sending, "ep", split_axis=0, concat_axis=0, tiled=True)
    my_docs = lax.dynamic_index_in_dim(query_docs, device, 0, keepdims=False)
    context = jnp.take(received, my_docs // pool_dev, axis=0)
    lengths = jnp.take(doc_lens, my_docs)
    positions = jnp.repeat(row_pos[:docs_per], doc_max, total_repeat_length=docs_per * doc_max)
    keys = rotate(context[:, :, :head_dim].reshape(docs_per * doc_max, head_dim), positions).astype(
        jnp.bfloat16
    )
    values = context[:, :, head_dim:].reshape(docs_per * doc_max, head_dim)
    valid = (jnp.arange(doc_max, dtype=jnp.int32)[None, :] < lengths[:, None]).reshape(
        docs_per * doc_max
    )
    return (keys, values, valid)


def project(attended, out_proj):
    lanes = lax.axis_size("tp")
    groups = lax.axis_size("ep")
    length = attended.shape[0]
    if lanes == groups:
        swap = [(e * lanes + t, t * lanes + e) for e in range(groups) for t in range(lanes)]
        block = lax.ppermute(attended, ("ep", "tp"), swap)
        tokens = lax.all_gather(block, "tp", axis=0, tiled=True)
    else:
        all_heads = lax.all_gather(attended, "tp", axis=1, tiled=True)
        split = jnp.swapaxes(all_heads.reshape(length, groups, -1), 0, 1)
        tokens = lax.all_to_all(split, "ep", split_axis=0, concat_axis=0, tiled=True)
        tokens = tokens.reshape(groups * length, -1)
    part = jnp.dot(tokens, out_proj, preferred_element_type=jnp.float32)
    return lax.psum_scatter(
        part.astype(jnp.bfloat16), "ep", scatter_dimension=0, tiled=True
    ).astype(jnp.float32)


def expert_kernel(
    tokens, w_in_hbm, w_out_hbm, result,
    w_in, w_out, sent, first, pair, second, acts,
    load_in, load_out, send_sem, recv_sem,
):
    count, rows, _ = tokens.shape
    lane = lax.axis_index("tp")
    chip = lane // 2
    core = lane % 2
    partner = chip * 2 + (1 - core)
    across = (1 - chip) * 2 + core
    loads_in = [
        pltpu.make_async_copy(w_in_hbm.at[e], w_in.at[e], load_in.at[e]) for e in range(count)
    ]
    loads_out = [
        pltpu.make_async_copy(w_out_hbm.at[e], w_out.at[e], load_out.at[e]) for e in range(count)
    ]
    for load in loads_in + loads_out:
        load.start()
    barrier = pltpu.get_barrier_semaphore()
    for other in (partner, across):
        pl.semaphore_signal(
            barrier, inc=1, device_id={"tp": other}, device_id_type=pl.DeviceIdType.MESH
        )
    pl.semaphore_wait(barrier, 2)

    def remote(kind, e, source, target, other):
        return pltpu.make_async_remote_copy(
            src_ref=source,
            dst_ref=target,
            send_sem=send_sem.at[kind, e],
            recv_sem=recv_sem.at[kind, e],
            device_id={"tp": other},
            device_id_type=pl.DeviceIdType.MESH,
        )

    copies = [
        [
            remote(0, e, sent.at[e, 1 - core], first.at[e], partner),
            remote(1, e, pair.at[e], second.at[e], across),
            remote(2, e, acts.at[e, core, chip], acts.at[e, core, chip], across),
            remote(3, e, acts.at[e, core, chip], acts.at[e, core, chip], partner),
            remote(4, e, acts.at[e, core, 1 - chip], acts.at[e, core, 1 - chip], partner),
        ]
        for e in range(count)
    ]

    def multiply_in(e):
        loads_in[e].wait()

        def block(i, carry):
            part = jnp.dot(
                tokens[e], w_in[e, i // 2, i % 2], preferred_element_type=jnp.float32
            )
            sent[e, i // 2, i % 2] = part.astype(jnp.bfloat16)
            return carry

        lax.fori_loop(0, 4, block, 0)
        copies[e][0].start()

    def add_pair(e):
        copies[e][0].wait_recv()
        total = sent[e, core, 1 - chip].astype(jnp.float32) + first[e, 1 - chip].astype(jnp.float32)
        pair[e] = total.astype(jnp.bfloat16)
        copies[e][1].start()

    def activate(e):
        copies[e][1].wait_recv()
        total = (
            sent[e, core, chip].astype(jnp.float32)
            + first[e, chip].astype(jnp.float32)
            + second[e].astype(jnp.float32)
        )
        half = total.shape[1] // 2
        gate = total[:, :half]
        acts[e, core, chip] = (gate / (1.0 + jnp.exp(-gate)) * total[:, half:]).astype(jnp.bfloat16)
        copies[e][2].start()
        copies[e][3].start()

    def forward(e):
        copies[e][2].wait_recv()
        copies[e][4].start()

    def multiply_out(e):
        copies[e][3].wait_recv()
        copies[e][4].wait_recv()
        loads_out[e].wait()
        joined = jnp.concatenate([acts[e, i % 2, i // 2] for i in range(4)], axis=1)
        result[e] = jnp.dot(joined, w_out[e], preferred_element_type=jnp.float32).astype(
            jnp.bfloat16
        )

    stages = (multiply_in, add_pair, activate, forward, multiply_out)
    delays = (0, 1, 3, 4, 5)
    for tick in range(count + delays[-1]):
        for stage, delay in zip(stages, delays):
            if 0 <= tick - delay < count:
                stage(tick - delay)
    for group in copies:
        for copy in group:
            copy.wait_send()


def feed_forward(arrived, w_gate_up, w_down):
    count, rows, width = arrived.shape
    lanes = lax.axis_size("tp")
    hidden_here = HID // lanes
    if lanes == 4:
        w_in = w_gate_up.reshape(count, width, 2, 2, 2, hidden_here)
        w_in = jnp.transpose(w_in, (0, 4, 3, 1, 2, 5)).reshape(
            count, 2, 2, width, 2 * hidden_here
        )
        bf16 = jnp.bfloat16
        return pl.pallas_call(
            expert_kernel,
            out_shape=jax.ShapeDtypeStruct(arrived.shape, bf16),
            in_specs=[
                pl.BlockSpec(memory_space=pltpu.VMEM),
                pl.BlockSpec(memory_space=pl.ANY),
                pl.BlockSpec(memory_space=pl.ANY),
            ],
            out_specs=pl.BlockSpec(memory_space=pltpu.VMEM),
            scratch_shapes=[
                pltpu.VMEM(w_in.shape, bf16),
                pltpu.VMEM(w_down.shape, bf16),
                pltpu.VMEM((count, 2, 2, rows, 2 * hidden_here), bf16),
                pltpu.VMEM((count, 2, rows, 2 * hidden_here), bf16),
                pltpu.VMEM((count, rows, 2 * hidden_here), bf16),
                pltpu.VMEM((count, rows, 2 * hidden_here), bf16),
                pltpu.VMEM((count, 2, 2, rows, hidden_here), bf16),
                pltpu.SemaphoreType.DMA((count,)),
                pltpu.SemaphoreType.DMA((count,)),
                pltpu.SemaphoreType.DMA((5, count)),
                pltpu.SemaphoreType.DMA((5, count)),
            ],
            compiler_params=pltpu.CompilerParams(
                collective_id=1, has_side_effects=True, vmem_limit_bytes=50 << 20
            ),
        )(arrived, w_in, w_down)
    term = jnp.einsum("erd,edgh->hegr", arrived, w_gate_up, preferred_element_type=jnp.float32)
    summed = lax.psum_scatter(
        term.astype(jnp.bfloat16), "tp", scatter_dimension=0, tiled=True
    ).astype(jnp.float32)
    activated = (jax.nn.silu(summed[:, :, 0]) * summed[:, :, 1]).astype(jnp.bfloat16)
    piece = lax.all_gather(activated, "tp", axis=0, tiled=True)
    return jnp.einsum(
        "her,ehd->erd", piece, w_down, preferred_element_type=jnp.float32
    ).astype(jnp.bfloat16)


def per_device(
    question_q,
    question_kv,
    doc_kv,
    doc_lens,
    query_docs,
    ctx_pos,
    hidden,
    out_proj,
    norm_gain,
    router_weight,
    w_gate_up,
    w_down,
    expert_ids,
):
    lanes = lax.axis_size("tp")
    groups = lax.axis_size("ep")
    lane = lax.axis_index("tp")
    device = lax.axis_index("ep")
    length, heads_here, head_dim = question_q.shape
    kv_heads = question_kv.shape[1]
    kv_pick = lane * kv_heads // lanes
    scale = head_dim ** (-0.5)
    docs_per = query_docs.shape[1]
    row_pos = lax.dynamic_index_in_dim(ctx_pos, device, 0, keepdims=False)
    question_pos = row_pos[docs_per] + jnp.arange(length, dtype=jnp.int32)
    queries = rotate(question_q, question_pos).astype(jnp.bfloat16)
    own_kv = lax.dynamic_index_in_dim(question_kv, kv_pick, 1, keepdims=False)
    own_keys = rotate(own_kv[:, 0], question_pos).astype(jnp.bfloat16)
    own_values = own_kv[:, 1]
    causal = jnp.arange(length)[:, None] >= jnp.arange(length)[None, :]
    doc_keys, doc_values, valid = fetch_context(
        doc_kv, doc_lens, query_docs, row_pos, device, kv_pick
    )
    keys = jnp.concatenate([doc_keys, own_keys], axis=0)
    values = jnp.concatenate([doc_values, own_values], axis=0)
    allowed = jnp.concatenate(
        [jnp.broadcast_to(valid[None, :], (length, valid.shape[0])), causal], axis=1
    )
    scores = jnp.einsum("ihd,jd->hij", queries, keys, preferred_element_type=jnp.float32) * scale
    scores = jnp.where(allowed[None], scores, -jnp.inf)
    ceiling = jnp.max(scores, axis=-1, keepdims=True)
    probs = jnp.exp(scores - ceiling)
    denominator = jnp.sum(probs, axis=-1, keepdims=True)
    mixed = jnp.einsum(
        "hij,jd->hid", probs.astype(jnp.bfloat16), values, preferred_element_type=jnp.float32
    )
    attended = (
        jnp.transpose(mixed / denominator, (1, 0, 2))
        .reshape(length, heads_here * head_dim)
        .astype(jnp.bfloat16)
    )
    width_here = hidden.shape[1]
    projected = project(attended, out_proj)
    residual_wide = narrow(hidden.astype(jnp.float32) + projected).astype(jnp.float32)
    gain = norm_gain.astype(jnp.float32)
    squares, logit_part = lax.psum(
        (
            jnp.sum(residual_wide * residual_wide, axis=1),
            jnp.dot(
                residual_wide * gain[None, :],
                router_weight.astype(jnp.float32),
                precision=lax.Precision.HIGHEST,
            ),
        ),
        "tp",
    )
    inv_rms = lax.rsqrt(squares / D + norm_eps)
    normed = (residual_wide * inv_rms[:, None] * gain[None, :]).astype(jnp.bfloat16)
    logits = logit_part * inv_rms[:, None]
    local_experts = w_gate_up.shape[0]
    capacity = length * expert_ids.shape[1] // (local_experts * groups)
    experts = logits.shape[1]
    chosen = jnp.any(expert_ids[:, :, None] == jnp.arange(experts, dtype=jnp.int32), axis=1)
    top = jnp.max(jnp.where(chosen, logits, -jnp.inf), axis=1, keepdims=True)
    raised = jnp.where(chosen, jnp.exp(jnp.where(chosen, logits - top, 0.0)), 0.0)
    mix = raised / jnp.sum(raised, axis=1, keepdims=True)
    mix_high = mix.astype(jnp.bfloat16)
    mix_low = (mix - mix_high.astype(jnp.float32)).astype(jnp.bfloat16)
    notes = jnp.concatenate([chosen.astype(jnp.bfloat16), mix_high, mix_low], axis=1)
    notes = jnp.pad(notes, ((0, 0), (0, -notes.shape[1] % 128)))
    packed = lax.all_gather(jnp.concatenate([normed, notes], axis=1), "ep", axis=0)
    normed_all = packed[:, :, :width_here]

    def mine(index):
        start = width_here + index * experts + device * local_experts
        return lax.dynamic_slice_in_dim(packed, start, local_experts, axis=2)

    member = mine(0) > 0
    share_high = jnp.swapaxes(mine(1), 1, 2)
    share_low = jnp.swapaxes(mine(2), 1, 2)
    earlier = jnp.arange(length)[:, None] > jnp.arange(length)[None, :]
    rank = jnp.einsum(
        "nm,sme->sen",
        earlier.astype(jnp.bfloat16),
        member.astype(jnp.bfloat16),
        preferred_element_type=jnp.float32,
    )
    seat = jnp.where(jnp.swapaxes(member, 1, 2), rank.astype(jnp.int32), -1)
    picks = (seat[:, :, None, :] == jnp.arange(capacity, dtype=jnp.int32)[:, None]).astype(
        jnp.bfloat16
    )
    arrived = jnp.einsum(
        "secn,snd->escd", picks, normed_all, preferred_element_type=jnp.float32
    ).astype(jnp.bfloat16)
    rows = groups * capacity
    arrived = arrived.reshape(local_experts, rows, width_here)
    expert_out = feed_forward(arrived, w_gate_up, w_down)
    weights = jnp.stack([picks * share_high[:, :, None, :], picks * share_low[:, :, None, :]])
    partial = jnp.einsum(
        "psecn,escd->snd",
        weights,
        expert_out.reshape(local_experts, groups, capacity, width_here),
        preferred_element_type=jnp.float32,
    )
    combined = lax.psum_scatter(
        partial.astype(jnp.bfloat16).reshape(groups * length, width_here),
        "ep",
        scatter_dimension=0,
        tiled=True,
    )
    return (residual_wide + combined.astype(jnp.float32)).astype(jnp.bfloat16)


def solution(mesh):
    placed = (
        P(("grp", "ep"), "tp", None),
        P(("grp", "ep"), None, None, None),
        P(("grp", "ep"), None, None, None, None),
        P("grp"),
        P("grp", None),
        P("grp", None),
        P(("grp", "ep"), "tp"),
        P("ep", "tp"),
        P("tp"),
        P("tp", None),
        P("ep", "tp", None, None),
        P("ep", None, "tp"),
        P(("grp", "ep"), None),
    )
    return jax.shard_map(
        per_device, mesh=mesh, in_specs=placed, out_specs=P(("grp", "ep"), "tp"), check_vma=False
    )
```

```python
import math

import jax
import jax.numpy as jnp
from jax import lax
from jax.experimental import pallas as pl
from jax.experimental.pallas import tpu as pltpu
from jax.sharding import PartitionSpec as P

D = 4096
HID = 1024


rope_theta = 1000000.0
norm_eps = 1e-06


def narrow(values):
    return lax.optimization_barrier(values.astype(jnp.bfloat16))


def rotate(values, positions):
    half = values.shape[-1] // 2
    freq = jnp.exp(
        jnp.arange(half, dtype=jnp.float32) * (-2.0 * math.log(rope_theta) / values.shape[-1])
    )
    angle = positions.astype(jnp.float32)[:, None] * freq[None, :]
    shape = (values.shape[0],) + (1,) * (values.ndim - 2) + (half,)
    cosine = jnp.cos(angle).reshape(shape)
    sine = jnp.sin(angle).reshape(shape)
    floats = values.astype(jnp.float32)
    first = floats[..., :half]
    second = floats[..., half:]
    return jnp.concatenate(
        [first * cosine - second * sine, second * cosine + first * sine], axis=-1
    )


def fetch_context(doc_kv, doc_lens, query_docs, row_pos, device, kv_pick):
    pool_dev, doc_max, kv_heads, pair, head_dim = doc_kv.shape
    docs_per = query_docs.shape[1]
    pool_head = lax.dynamic_index_in_dim(doc_kv, kv_pick, 2, keepdims=False).reshape(
        pool_dev, doc_max, pair * head_dim
    )
    held = device * pool_dev + jnp.arange(pool_dev, dtype=jnp.int32)
    wanted = jnp.sum((query_docs[:, :, None] == held[None, None, :]).astype(jnp.float32), axis=1)
    sending = jnp.einsum(
        "rl,lkc->rkc", wanted.astype(jnp.bfloat16), pool_head, preferred_element_type=jnp.float32
    ).astype(jnp.bfloat16)
    received = lax.all_to_all(sending, "ep", split_axis=0, concat_axis=0, tiled=True)
    my_docs = lax.dynamic_index_in_dim(query_docs, device, 0, keepdims=False)
    context = jnp.take(received, my_docs // pool_dev, axis=0)
    lengths = jnp.take(doc_lens, my_docs)
    positions = jnp.repeat(row_pos[:docs_per], doc_max, total_repeat_length=docs_per * doc_max)
    keys = rotate(context[:, :, :head_dim].reshape(docs_per * doc_max, head_dim), positions).astype(
        jnp.bfloat16
    )
    values = context[:, :, head_dim:].reshape(docs_per * doc_max, head_dim)
    valid = (jnp.arange(doc_max, dtype=jnp.int32)[None, :] < lengths[:, None]).reshape(
        docs_per * doc_max
    )
    return (keys, values, valid)


def project(attended, out_proj, w_gate_up):
    lanes = lax.axis_size("tp")
    groups = lax.axis_size("ep")
    length = attended.shape[0]
    halves = None
    if lanes == 4:
        attended, whole = lax.optimization_barrier((attended, w_gate_up))
        halves = (whole[:, :, 0], whole[:, :, 1])
    if lanes == groups:
        swap = [(e * lanes + t, t * lanes + e) for e in range(groups) for t in range(lanes)]
        block = lax.ppermute(attended, ("ep", "tp"), swap)
        tokens = lax.all_gather(block, "tp", axis=0, tiled=True)
    else:
        all_heads = lax.all_gather(attended, "tp", axis=1, tiled=True)
        split = jnp.swapaxes(all_heads.reshape(length, groups, -1), 0, 1)
        tokens = lax.all_to_all(split, "ep", split_axis=0, concat_axis=0, tiled=True)
        tokens = tokens.reshape(groups * length, -1)
    if halves is not None:
        tokens, halves = lax.optimization_barrier((tokens, halves))
    part = jnp.dot(tokens, out_proj, preferred_element_type=jnp.float32)
    summed = lax.psum_scatter(
        part.astype(jnp.bfloat16), "ep", scatter_dimension=0, tiled=True
    ).astype(jnp.float32)
    return summed, halves


def expert_kernel(
    tokens, w_gate_hbm, w_up_hbm, w_out_hbm, result,
    w_gate, w_up, w_out, sent, first, pair, second, acts,
    load_in, load_out, send_sem, recv_sem,
):
    count, rows, _ = tokens.shape
    lane = lax.axis_index("tp")
    chip = lane // 2
    core = lane % 2
    partner = chip * 2 + (1 - core)
    across = (1 - chip) * 2 + core
    loads_in = [
        pltpu.make_async_copy(source.at[e], target.at[e], load_in.at[kind, e])
        for e in range(count)
        for kind, (source, target) in enumerate(((w_gate_hbm, w_gate), (w_up_hbm, w_up)))
    ]
    loads_out = [
        pltpu.make_async_copy(w_out_hbm.at[e], w_out.at[e], load_out.at[e]) for e in range(count)
    ]
    for load in loads_in + loads_out:
        load.start()
    barrier = pltpu.get_barrier_semaphore()
    for other in (partner, across):
        pl.semaphore_signal(
            barrier, inc=1, device_id={"tp": other}, device_id_type=pl.DeviceIdType.MESH
        )
    pl.semaphore_wait(barrier, 2)

    def remote(kind, e, source, target, other):
        return pltpu.make_async_remote_copy(
            src_ref=source,
            dst_ref=target,
            send_sem=send_sem.at[kind, e],
            recv_sem=recv_sem.at[kind, e],
            device_id={"tp": other},
            device_id_type=pl.DeviceIdType.MESH,
        )

    copies = [
        [
            remote(0, e, sent.at[e, 1 - core], first.at[e], partner),
            remote(1, e, pair.at[e], second.at[e], across),
            remote(2, e, acts.at[e, core, chip], acts.at[e, core, chip], across),
            remote(3, e, acts.at[e, core, chip], acts.at[e, core, chip], partner),
            remote(4, e, acts.at[e, core, 1 - chip], acts.at[e, core, 1 - chip], partner),
        ]
        for e in range(count)
    ]

    def multiply_in(e):
        loads_in[2 * e].wait()
        loads_in[2 * e + 1].wait()
        width = w_gate.shape[2] // 4

        def block(i, carry):
            columns = pl.ds(pl.multiple_of(i * width, width), width)
            for kind, weights in enumerate((w_gate, w_up)):
                part = jnp.dot(
                    tokens[e], weights[e, :, columns], preferred_element_type=jnp.float32
                )
                sent[e, i % 2, i // 2, :, kind * width : (kind + 1) * width] = part.astype(
                    jnp.bfloat16
                )
            return carry

        lax.fori_loop(0, 4, block, 0)
        copies[e][0].start()

    def add_pair(e):
        copies[e][0].wait_recv()
        total = sent[e, core, 1 - chip].astype(jnp.float32) + first[e, 1 - chip].astype(jnp.float32)
        pair[e] = total.astype(jnp.bfloat16)
        copies[e][1].start()

    def activate(e):
        copies[e][1].wait_recv()
        total = (
            sent[e, core, chip].astype(jnp.float32)
            + first[e, chip].astype(jnp.float32)
            + second[e].astype(jnp.float32)
        )
        half = total.shape[1] // 2
        gate = total[:, :half]
        acts[e, core, chip] = (gate / (1.0 + jnp.exp(-gate)) * total[:, half:]).astype(jnp.bfloat16)
        copies[e][2].start()
        copies[e][3].start()

    def forward(e):
        copies[e][2].wait_recv()
        copies[e][4].start()

    def multiply_out(e):
        copies[e][3].wait_recv()
        copies[e][4].wait_recv()
        loads_out[e].wait()
        joined = jnp.concatenate([acts[e, i % 2, i // 2] for i in range(4)], axis=1)
        result[e] = jnp.dot(joined, w_out[e], preferred_element_type=jnp.float32).astype(
            jnp.bfloat16
        )

    stages = (multiply_in, add_pair, activate, forward, multiply_out)
    delays = (0, 1, 3, 4, 5)
    for tick in range(count + delays[-1]):
        for stage, delay in zip(stages, delays):
            if 0 <= tick - delay < count:
                stage(tick - delay)
    for group in copies:
        for copy in group:
            copy.wait_send()


def feed_forward(arrived, w_gate_up, halves, w_down):
    count, rows, width = arrived.shape
    lanes = lax.axis_size("tp")
    hidden_here = HID // lanes
    if lanes == 4:
        w_gate, w_up = halves
        bf16 = jnp.bfloat16
        return pl.pallas_call(
            expert_kernel,
            out_shape=jax.ShapeDtypeStruct(arrived.shape, bf16),
            in_specs=[
                pl.BlockSpec(memory_space=pltpu.VMEM),
                pl.BlockSpec(memory_space=pl.ANY),
                pl.BlockSpec(memory_space=pl.ANY),
                pl.BlockSpec(memory_space=pl.ANY),
            ],
            out_specs=pl.BlockSpec(memory_space=pltpu.VMEM),
            scratch_shapes=[
                pltpu.VMEM(w_gate.shape, bf16),
                pltpu.VMEM(w_up.shape, bf16),
                pltpu.VMEM(w_down.shape, bf16),
                pltpu.VMEM((count, 2, 2, rows, 2 * hidden_here), bf16),
                pltpu.VMEM((count, 2, rows, 2 * hidden_here), bf16),
                pltpu.VMEM((count, rows, 2 * hidden_here), bf16),
                pltpu.VMEM((count, rows, 2 * hidden_here), bf16),
                pltpu.VMEM((count, 2, 2, rows, hidden_here), bf16),
                pltpu.SemaphoreType.DMA((2, count)),
                pltpu.SemaphoreType.DMA((count,)),
                pltpu.SemaphoreType.DMA((5, count)),
                pltpu.SemaphoreType.DMA((5, count)),
            ],
            compiler_params=pltpu.CompilerParams(
                collective_id=1, has_side_effects=True, vmem_limit_bytes=50 << 20
            ),
        )(arrived, w_gate, w_up, w_down)
    term = jnp.einsum("erd,edgh->hegr", arrived, w_gate_up, preferred_element_type=jnp.float32)
    summed = lax.psum_scatter(
        term.astype(jnp.bfloat16), "tp", scatter_dimension=0, tiled=True
    ).astype(jnp.float32)
    activated = (jax.nn.silu(summed[:, :, 0]) * summed[:, :, 1]).astype(jnp.bfloat16)
    piece = lax.all_gather(activated, "tp", axis=0, tiled=True)
    return jnp.einsum(
        "her,ehd->erd", piece, w_down, preferred_element_type=jnp.float32
    ).astype(jnp.bfloat16)


def per_device(
    question_q,
    question_kv,
    doc_kv,
    doc_lens,
    query_docs,
    ctx_pos,
    hidden,
    out_proj,
    norm_gain,
    router_weight,
    w_gate_up,
    w_down,
    expert_ids,
):
    lanes = lax.axis_size("tp")
    groups = lax.axis_size("ep")
    lane = lax.axis_index("tp")
    device = lax.axis_index("ep")
    length, heads_here, head_dim = question_q.shape
    kv_heads = question_kv.shape[1]
    kv_pick = lane * kv_heads // lanes
    scale = head_dim ** (-0.5)
    docs_per = query_docs.shape[1]
    row_pos = lax.dynamic_index_in_dim(ctx_pos, device, 0, keepdims=False)
    question_pos = row_pos[docs_per] + jnp.arange(length, dtype=jnp.int32)
    queries = rotate(question_q, question_pos).astype(jnp.bfloat16)
    own_kv = lax.dynamic_index_in_dim(question_kv, kv_pick, 1, keepdims=False)
    own_keys = rotate(own_kv[:, 0], question_pos).astype(jnp.bfloat16)
    own_values = own_kv[:, 1]
    causal = jnp.arange(length)[:, None] >= jnp.arange(length)[None, :]
    doc_keys, doc_values, valid = fetch_context(
        doc_kv, doc_lens, query_docs, row_pos, device, kv_pick
    )
    keys = jnp.concatenate([doc_keys, own_keys], axis=0)
    values = jnp.concatenate([doc_values, own_values], axis=0)
    allowed = jnp.concatenate(
        [jnp.broadcast_to(valid[None, :], (length, valid.shape[0])), causal], axis=1
    )
    scores = jnp.einsum("ihd,jd->hij", queries, keys, preferred_element_type=jnp.float32) * scale
    scores = jnp.where(allowed[None], scores, -jnp.inf)
    ceiling = jnp.max(scores, axis=-1, keepdims=True)
    probs = jnp.exp(scores - ceiling)
    denominator = jnp.sum(probs, axis=-1, keepdims=True)
    mixed = jnp.einsum(
        "hij,jd->hid", probs.astype(jnp.bfloat16), values, preferred_element_type=jnp.float32
    )
    attended = (
        jnp.transpose(mixed / denominator, (1, 0, 2))
        .reshape(length, heads_here * head_dim)
        .astype(jnp.bfloat16)
    )
    width_here = hidden.shape[1]
    projected, halves = project(attended, out_proj, w_gate_up)
    residual_wide = narrow(hidden.astype(jnp.float32) + projected).astype(jnp.float32)
    gain = norm_gain.astype(jnp.float32)
    squares, logit_part = lax.psum(
        (
            jnp.sum(residual_wide * residual_wide, axis=1),
            jnp.dot(
                residual_wide * gain[None, :],
                router_weight.astype(jnp.float32),
                precision=lax.Precision.HIGHEST,
            ),
        ),
        "tp",
    )
    inv_rms = lax.rsqrt(squares / D + norm_eps)
    normed = (residual_wide * inv_rms[:, None] * gain[None, :]).astype(jnp.bfloat16)
    logits = logit_part * inv_rms[:, None]
    local_experts = w_gate_up.shape[0]
    capacity = length * expert_ids.shape[1] // (local_experts * groups)
    experts = logits.shape[1]
    chosen = jnp.any(expert_ids[:, :, None] == jnp.arange(experts, dtype=jnp.int32), axis=1)
    top = jnp.max(jnp.where(chosen, logits, -jnp.inf), axis=1, keepdims=True)
    raised = jnp.where(chosen, jnp.exp(jnp.where(chosen, logits - top, 0.0)), 0.0)
    mix = raised / jnp.sum(raised, axis=1, keepdims=True)
    mix_high = mix.astype(jnp.bfloat16)
    mix_low = (mix - mix_high.astype(jnp.float32)).astype(jnp.bfloat16)
    notes = jnp.concatenate([chosen.astype(jnp.bfloat16), mix_high, mix_low], axis=1)
    notes = jnp.pad(notes, ((0, 0), (0, -notes.shape[1] % 128)))
    packed = lax.all_gather(jnp.concatenate([normed, notes], axis=1), "ep", axis=0)
    normed_all = packed[:, :, :width_here]

    def mine(index):
        start = width_here + index * experts + device * local_experts
        return lax.dynamic_slice_in_dim(packed, start, local_experts, axis=2)

    member = mine(0) > 0
    share_high = jnp.swapaxes(mine(1), 1, 2)
    share_low = jnp.swapaxes(mine(2), 1, 2)
    earlier = jnp.arange(length)[:, None] > jnp.arange(length)[None, :]
    rank = jnp.einsum(
        "nm,sme->sen",
        earlier.astype(jnp.bfloat16),
        member.astype(jnp.bfloat16),
        preferred_element_type=jnp.float32,
    )
    seat = jnp.where(jnp.swapaxes(member, 1, 2), rank.astype(jnp.int32), -1)
    picks = (seat[:, :, None, :] == jnp.arange(capacity, dtype=jnp.int32)[:, None]).astype(
        jnp.bfloat16
    )
    arrived = jnp.einsum(
        "secn,snd->escd", picks, normed_all, preferred_element_type=jnp.float32
    ).astype(jnp.bfloat16)
    rows = groups * capacity
    arrived = arrived.reshape(local_experts, rows, width_here)
    expert_out = feed_forward(arrived, w_gate_up, halves, w_down)
    weights = jnp.stack([picks * share_high[:, :, None, :], picks * share_low[:, :, None, :]])
    partial = jnp.einsum(
        "psecn,escd->snd",
        weights,
        expert_out.reshape(local_experts, groups, capacity, width_here),
        preferred_element_type=jnp.float32,
    )
    combined = lax.psum_scatter(
        partial.astype(jnp.bfloat16).reshape(groups * length, width_here),
        "ep",
        scatter_dimension=0,
        tiled=True,
    )
    return (residual_wide + combined.astype(jnp.float32)).astype(jnp.bfloat16)


def solution(mesh):
    placed = (
        P(("grp", "ep"), "tp", None),
        P(("grp", "ep"), None, None, None),
        P(("grp", "ep"), None, None, None, None),
        P("grp"),
        P("grp", None),
        P("grp", None),
        P(("grp", "ep"), "tp"),
        P("ep", "tp"),
        P("tp"),
        P("tp", None),
        P("ep", "tp", None, None),
        P("ep", None, "tp"),
        P(("grp", "ep"), None),
    )
    return jax.shard_map(
        per_device, mesh=mesh, in_specs=placed, out_specs=P(("grp", "ep"), "tp"), check_vma=False
    )
```
